32 devices in a mesh: tgrp: 4 (over y, x), inner: 8 (over z, core).
Axes of the slice: x: 2, y: 2, z: 4, core: 2. Of those that a mesh axis runs over, the one named last changes fastest.
Arguments:
- observations: float32 [1024, 128, 256], P(('tgrp', 'inner')), may hold values from -16 to 16
- obs_mask: int32 [1024, 128, 256], P(('tgrp', 'inner')), may hold values 0 or 1
- obs_precision: float32 [1024], P(('tgrp', 'inner')), may hold values from 0.5 to 4
- range_class: int32 [128, 256], replicated, may hold values from 0 to 7
- class_kappa: float32 [8], replicated, may hold values from 0.5 to 4
- time_precision: float32 [1024, 1024], replicated, may hold values from -1 to 3, as said below
Outputs:
- solution_field: float32 [1024, 128, 256], P(('tgrp', 'inner'))
- residual: float32 [1024, 128, 256], P(('tgrp', 'inner'))
The draws below stay inside these ranges and needn't reach their ends.
Inputs may be any that keep to these rules, and one draw needn't show every extreme that they name: `time_precision`: symmetric positive definite.
All inputs are finite; a program needn't handle non-finite values. No bound on the sum of `obs_mask` on one device may be relied on, other than what follows from the above.
Results may differ from the reference program's by a relative error of at most 0.00021.
Values sent between devices are 32-bit elements; how exact they have to be, the bound alone decides.
No kernel may reach another device: no remote copies, remote signals or barrier semaphores. Data moves between devices by JAX's collectives and lax.ppermute only.
A program may use at most 512 MiB of HBM per device.

```python
import math
import jax
import jax.numpy as jnp
from jax import lax

TLEN = 1024
NR = 128
NC = 256
NCLASS = 8
ITERS = 2


def draw_time_precision(key, part):
    key_amp, key_diag, key_noise = jax.random.split(jax.random.fold_in(key, 11), 3)
    amplitude = jnp.exp(jax.random.uniform(key_amp, (TLEN,), jnp.float32, jnp.log(0.1), jnp.log(0.3)))
    diagonal = jax.random.uniform(key_diag, (TLEN,), jnp.float32, 1.5, 2.5)
    noise = jax.random.uniform(key_noise, (TLEN, TLEN), jnp.float32, -1.0, 1.0)
    noise = 0.25 * (noise + noise.T) / float(TLEN) ** 0.5
    steps = jnp.arange(TLEN).astype(jnp.float32)
    distance = jnp.abs(steps[:, None] - steps[None, :])
    kernel = jnp.exp(-distance / (TLEN / 8.0))
    ident = jnp.eye(TLEN, dtype=jnp.float32)
    return amplitude[:, None] * amplitude[None, :] * kernel + noise * (1.0 - ident) + diagonal[:, None] * ident


def plant(array, own_key, least, high):
    index_at = [jax.random.randint(jax.random.fold_in(own_key, axis), (), 0, length) for axis, length in enumerate(array.shape)]
    main_axis = array.shape.index(max(array.shape))
    beside = index_at[:main_axis] + [(index_at[main_axis] + 1) % array.shape[main_axis]] + index_at[main_axis + 1:]
    return array.at[tuple(index_at)].set(least).at[tuple(beside)].set(high)


def levels(rng, shape, cuts, smallest, high):
    def one(dim, shards_of):
        steps = jax.random.uniform(jax.random.fold_in(jax.random.fold_in(rng, 6), dim), (shards_of,), jnp.float32, smallest / len(cuts), high / len(cuts))
        return jnp.repeat(jnp.exp(steps), shape[dim] // shards_of).reshape((-1,) + (1,) * (len(shape) - dim - 1))

    level = one(*cuts[0])
    for cut in cuts[1:]:
        level = level * one(*cut)
    return level


def gaussian(key, extent, spread, reach, pieces=(), kind=jnp.bfloat16):
    array = jax.random.normal(key, extent, jnp.float32) * spread
    if len(pieces) > 0:
        array = levels(key, extent, pieces, -0.22, 0.18) * array
    return jnp.clip(array, min=-reach, max=reach).astype(kind)


def setup_inputs(seed: int = 0) -> dict:
    streams_of = jax.random.split(jax.random.key(seed), 7)
    return {
        "observations": gaussian(streams_of[0], (TLEN, NR, NC), 4.0, 16.0, ((0, 32),), jnp.float32),
        "obs_mask": plant((jax.random.randint(streams_of[1], (TLEN, NR, NC), 0, 2) < 1).astype(jnp.int32), jax.random.fold_in(streams_of[1], 1), 0, 1),
        "obs_precision": jnp.clip(jnp.exp(math.log(4.0) - 2.0794415 * jax.random.uniform(streams_of[2], (TLEN,), jnp.float32) ** levels(streams_of[2], (TLEN,), ((0, 32),), -0.2, 0.2)), 0.5, 4.0),
        "range_class": plant(jax.random.randint(streams_of[3], (NR, NC), 0, NCLASS), jax.random.fold_in(streams_of[3], 1), 0, NCLASS - 1).astype(jnp.int32),
        "class_kappa": jnp.clip(jnp.exp(jax.random.uniform(streams_of[4], (NCLASS,), jnp.float32, math.log(0.5), math.log(4.0))), 0.5, 4.0),
        "time_precision": draw_time_precision(jax.random.fold_in(streams_of[6], 71), 0),
    }


def spatial(field, kappa_sq):
    padded = jnp.pad(field, ((0, 0), (1, 1), (1, 1)))
    edges = padded[:, 2:, 1:-1] + padded[:, :-2, 1:-1] + padded[:, 1:-1, 2:] + padded[:, 1:-1, :-2]
    corners = padded[:, 2:, 2:] + padded[:, 2:, :-2] + padded[:, :-2, 2:] + padded[:, :-2, :-2]
    return (kappa_sq + 20.0 / 6.0) * field - (4.0 * edges + corners) / 6.0


def reference(observations, obs_mask, obs_precision, range_class, class_kappa, time_precision):
    kappa_sq = class_kappa[range_class]
    weight = obs_precision[:, None, None] * obs_mask.astype(jnp.float32)
    right_side = weight * observations

    def operate(field):
        shaped = spatial(field, kappa_sq)
        product = jnp.dot(time_precision, shaped.reshape(TLEN, NR * NC), precision=lax.Precision.HIGHEST, preferred_element_type=jnp.float32)
        return product.reshape(field.shape) + weight * field

    solution_field = jnp.zeros_like(right_side)
    residual = right_side
    direction = right_side
    norm_now = jnp.sum(residual * residual)
    for step in range(ITERS):
        image = operate(direction)
        alpha = norm_now / jnp.sum(direction * image)
        solution_field = solution_field + alpha * direction
        residual = residual - alpha * image
        norm_next = jnp.sum(residual * residual)
        direction = residual + (norm_next / norm_now) * direction
        norm_now = norm_next
    return solution_field, residual
```

```python
import functools

import jax
import jax.numpy as jnp
from jax import lax
from jax.experimental import pallas as pl
from jax.experimental.pallas import tpu as pltpu
from jax.sharding import PartitionSpec as P

ITERS = 2
LANES = 128
SUBS = 8
AXES = ("tgrp", "inner")
F32 = jnp.float32
BF16 = jnp.bfloat16


def spatial(field, kappa_sq):
    padded = jnp.pad(field, ((0, 0), (1, 1), (1, 1)))
    edges = padded[:, 2:, 1:-1] + padded[:, :-2, 1:-1] + padded[:, 1:-1, 2:] + padded[:, 1:-1, :-2]
    corners = padded[:, 2:, 2:] + padded[:, 2:, :-2] + padded[:, :-2, 2:] + padded[:, :-2, :-2]
    return (kappa_sq + 20.0 / 6.0) * field - (4.0 * edges + corners) / 6.0


def squares(residual):
    return lax.psum(jnp.sum(residual * residual), AXES)


def general(observations, obs_mask, obs_precision, range_class, class_kappa, time_precision):
    devices = lax.axis_size("tgrp") * lax.axis_size("inner")
    steps_dev, rows, cols = observations.shape
    remain = rows * cols // devices
    total_len = time_precision.shape[0]
    levels = jnp.arange(class_kappa.shape[0], dtype=jnp.int32)
    kappa_sq = jnp.sum(
        jnp.where(
            range_class[None, :, :] == levels[:, None, None], class_kappa[:, None, None], 0.0
        ),
        axis=0,
    )
    weight = obs_precision[:, None, None] * obs_mask.astype(F32)
    right_side = weight * observations
    solution_field = jnp.zeros_like(right_side)
    residual = right_side
    direction = right_side
    norm_now = squares(residual)
    for step in range(ITERS):
        blocks = spatial(direction, kappa_sq).reshape(steps_dev, devices, remain)
        moved = lax.all_to_all(blocks.transpose(1, 0, 2), AXES, 0, 0, tiled=True)
        product = jnp.dot(
            time_precision,
            moved.reshape(total_len, remain),
            precision=lax.Precision.HIGHEST,
            preferred_element_type=F32,
        )
        back = lax.all_to_all(product.reshape(devices, steps_dev, remain), AXES, 0, 0, tiled=True)
        image = back.transpose(1, 0, 2).reshape(steps_dev, rows, cols) + weight * direction
        alpha = norm_now / lax.psum(jnp.sum(direction * image), AXES)
        solution_field = solution_field + alpha * direction
        residual = residual - alpha * image
        if step + 1 < ITERS:
            norm_next = squares(residual)
            direction = residual + norm_next / norm_now * direction
            norm_now = norm_next
    return (solution_field, residual)


def strip_order(groups, members):
    ring = [g ^ (g >> 1) for g in range(groups)]
    order = []
    for plane in range(members // 2):
        for g in ring if plane % 2 == 0 else ring[::-1]:
            order += [g * members + plane * 2, g * members + plane * 2 + 1]
    return order


def global_sum(part, devices):
    step = 1
    while step < devices:
        pairs = [(a, a ^ step) for a in range(devices)]
        part = part + lax.ppermute(part, AXES, pairs)
        step *= 2
    return part


def kappa_of(classes, table_ref):
    field = jnp.zeros(classes.shape, F32)
    for level in range(table_ref.shape[0]):
        field = jnp.where(classes == level, table_ref[level], field)
    return field + 20.0 / 6.0


def neighbours(edge, centre, column, cols):
    both = 4.0 * centre + edge
    left = jnp.where(column == 0, 0.0, pltpu.roll(both, 1, both.ndim - 1))
    right = jnp.where(column == cols - 1, 0.0, pltpu.roll(both, cols - 1, both.ndim - 1))
    return 4.0 * edge + left + right


def forward_kernel(order_ref, *refs):
    s_ref, bt, kap = refs[-3:]
    table_ref, cls_ref, prec_ref = refs[-6:-3]
    halves = (len(refs) - 6) // 2
    obs, mask = refs[:halves], refs[halves : 2 * halves]
    devices, strip, subs, cols = s_ref.shape
    rows = devices * strip

    @pl.when(pl.program_id(0) == 0)
    def _():
        kap[...] = kappa_of(cls_ref[...], table_ref)
        bt[0] = jnp.zeros_like(bt[0])
        bt[rows + 1] = jnp.zeros_like(bt[0])

    prec = prec_ref[...]

    def load(k, carry):
        for q in range(strip):
            r = k * strip + q
            for h in range(halves):
                at = pl.ds(r, subs, stride=rows)
                o = obs[h].reshape(subs * rows, LANES)[at, :]
                m = mask[h].reshape(subs * rows, LANES)[at, :]
                bt[r + 1, :, h * LANES : (h + 1) * LANES] = prec * m.astype(F32) * o
        return carry

    lax.fori_loop(0, devices, load, 0)
    column = lax.broadcasted_iota(jnp.int32, (subs, cols), 1)

    def stencil(k, carry):
        dest = order_ref[k]
        for q in range(strip):
            r = k * strip + q
            centre = bt[r + 1]
            around = neighbours(bt[r] + bt[r + 2], centre, column, cols)
            s_ref[dest, q] = kap[pl.ds(r, 1), :] * centre - around * (1.0 / 6.0)
        return carry

    lax.fori_loop(0, devices, stencil, 0)


def split_kernel(t_ref, hi_ref, lo_ref):
    value = t_ref[...]
    hi = value.astype(BF16)
    hi_ref[...] = hi
    lo_ref[...] = (value - hi.astype(F32)).astype(BF16)


def times(hi_ref, lo_ref, xh, xl, out_ref):
    devices, _, steps, cols = out_ref.shape
    total = devices * steps
    tile = min(total, 256)

    def body(m, carry):
        at = pl.ds(pl.multiple_of(m * tile, tile), tile)
        hi, lo = hi_ref[at, :], lo_ref[at, :]
        dot = functools.partial(jnp.dot, preferred_element_type=F32)
        acc = dot(hi, xl[...]) + dot(lo, xh[...]) + dot(hi, xh[...])
        out_ref[pl.ds(m * (tile // steps), tile // steps), 0] = acc.reshape(tile // steps, steps, cols)
        return carry

    lax.fori_loop(0, total // tile, body, 0)


def first_kernel(hi_ref, lo_ref, s_ref, u_ref, xh, xl):
    devices, _, steps, cols = s_ref.shape
    value = s_ref[...].reshape(devices * steps, cols)
    hi = value.astype(BF16)
    xh[...] = hi
    xl[...] = (value - hi.astype(F32)).astype(BF16)
    times(hi_ref, lo_ref, xh, xl, u_ref)


def second_kernel(
    hi_ref, lo_ref, table_ref, cls_ref, dia_ref, up_ref, down_ref, above_ref, u_ref, below_ref, s_ref, v_ref, xh, xl
):
    q = pl.program_id(0)
    last = pl.num_programs(0) - 1
    devices, _, steps, cols = s_ref.shape
    kap = kappa_of(cls_ref[pl.ds(q, 1), :], table_ref)
    some = max(1, 64 // steps)
    size = some * steps
    column = lax.broadcasted_iota(jnp.int32, (size, cols), 1)

    def body(i, carry):
        at = pl.ds(i * some, some)
        flat = lambda value: value.reshape(size, cols)
        above = jnp.where(q == 0, flat(up_ref[at]), flat(above_ref[at, 0]))
        below = jnp.where(q == last, flat(down_ref[at]), flat(below_ref[at, 0]))
        centre = flat(u_ref[at, 0])
        rows = pl.ds(pl.multiple_of(i * size, size), size)
        dia = dia_ref[rows, :]
        dia = jnp.concatenate([dia] * (cols // LANES), axis=1)
        value = kap * centre - neighbours(above + below, centre, column, cols) * (1.0 / 6.0)
        value = value + dia * flat(s_ref[at, 0])
        hi = value.astype(BF16)
        xh[rows, :] = hi
        xl[rows, :] = (value - hi.astype(F32)).astype(BF16)
        return carry

    lax.fori_loop(0, devices // some, body, 0)
    times(hi_ref, lo_ref, xh, xl, v_ref)


def total_of(ref, at=0):
    return jnp.sum(ref[at * SUBS : (at + 1) * SUBS, :], keepdims=True)


def each_row(order_ref, obs_ref, mask_ref, prec_ref, fields, body, carry):
    devices, strip, subs, _ = fields.shape
    rows = devices * strip
    prec = prec_ref[...]

    def one(k, carry):
        dest = order_ref[k]
        for q in range(strip):
            at = pl.ds(k * strip + q, subs, stride=rows)
            weight = prec * mask_ref.reshape(subs * rows, LANES)[at, :].astype(F32)
            b = weight * obs_ref.reshape(subs * rows, LANES)[at, :]
            z = fields[dest, q] + prec * b
            carry = body(at, dest, q, b, z, weight, carry)
        return carry

    return lax.fori_loop(0, devices, one, carry)


def is_first():
    return jnp.logical_and(pl.program_id(0) == 0, pl.program_id(1) == 0)


def moments_kernel(order_ref, obs_ref, mask_ref, prec_ref, u_ref, sums_ref):
    @pl.when(is_first())
    def _():
        sums_ref[...] = jnp.zeros_like(sums_ref)

    def body(at, dest, q, b, z, weight, carry):
        return carry[0] + b * b, carry[1] + b * z

    zero = jnp.zeros((SUBS, LANES), F32)
    bb, bz = each_row(order_ref, obs_ref, mask_ref, prec_ref, u_ref, body, (zero, zero))
    sums_ref[:SUBS] += bb
    sums_ref[SUBS:] += bz


def residual_kernel(order_ref, obs_ref, mask_ref, prec_ref, u_ref, sums_ref, out_ref):
    @pl.when(is_first())
    def _():
        out_ref[...] = jnp.zeros_like(out_ref)

    alpha = total_of(sums_ref) / total_of(sums_ref, 1)

    def body(at, dest, q, b, z, weight, carry):
        r1 = b - alpha * z
        return carry + r1 * r1

    zero = jnp.zeros((SUBS, LANES), F32)
    out_ref[...] += each_row(order_ref, obs_ref, mask_ref, prec_ref, u_ref, body, zero)


def direction_kernel(order_ref, obs_ref, mask_ref, prec_ref, u_ref, sums_ref, new_ref, d_ref, out_ref):
    @pl.when(is_first())
    def _():
        out_ref[...] = jnp.zeros_like(out_ref)

    alpha = total_of(sums_ref) / total_of(sums_ref, 1)
    beta = total_of(new_ref) / total_of(sums_ref)

    def body(at, dest, q, b, z, weight, carry):
        d1 = b - alpha * z + beta * b
        d_ref[dest, q] = d1
        return carry + d1 * ((1.0 + beta) * z - alpha * (weight * z))

    zero = jnp.zeros((SUBS, LANES), F32)
    out_ref[...] += each_row(order_ref, obs_ref, mask_ref, prec_ref, u_ref, body, zero)


def denominator_kernel(d_ref, v_ref, sums_ref, part_ref, out_ref):
    @pl.when(pl.program_id(0) == 0)
    def _():
        out_ref[...] = part_ref[...]

    alpha = total_of(sums_ref) / total_of(sums_ref, 1)
    product = d_ref[...] * v_ref[...]
    product = product.reshape(-1, SUBS, product.shape[-1]).sum(0)
    acc = product[:, :LANES]
    for h in range(1, product.shape[-1] // LANES):
        acc = acc + product[:, h * LANES : (h + 1) * LANES]
    out_ref[...] -= alpha * acc


def final_kernel(
    order_ref, obs_ref, mask_ref, prec_ref, u_ref, v_ref, sums_ref, new_ref, den_ref, x_ref, r_ref
):
    alpha = total_of(sums_ref) / total_of(sums_ref, 1)
    beta = total_of(new_ref) / total_of(sums_ref)
    step = total_of(new_ref) / total_of(den_ref)
    subs, rows, _ = x_ref.shape

    def body(at, dest, q, b, z, weight, carry):
        r1 = b - alpha * z
        d1 = r1 + beta * b
        image = (1.0 + beta) * z - alpha * (v_ref[dest, q] + weight * z)
        x_ref.reshape(subs * rows, LANES)[at, :] = alpha * b + step * d1
        r_ref.reshape(subs * rows, LANES)[at, :] = r1 - step * image
        return carry

    each_row(order_ref, obs_ref, mask_ref, prec_ref, u_ref, body, 0)


def fast(observations, obs_mask, obs_precision, range_class, class_kappa, time_precision):
    groups, members = lax.axis_size("tgrp"), lax.axis_size("inner")
    devices = groups * members
    steps, rows, cols = observations.shape
    total = time_precision.shape[0]
    strip = rows // devices
    halves = cols // LANES
    order = strip_order(groups, members)
    order_arr = jnp.array(order, jnp.int32)
    place = [order.index(d) for d in range(devices)]
    me = lax.axis_index(AXES)
    my_strip = jnp.array(place, jnp.int32)[me]
    field = jax.ShapeDtypeStruct((devices, strip, steps, cols), F32)
    small = jax.ShapeDtypeStruct((SUBS, LANES), F32)
    smem = pl.BlockSpec(memory_space=pltpu.SMEM)
    big = pltpu.CompilerParams(vmem_limit_bytes=60 * 2**20)

    prec = jnp.broadcast_to(obs_precision[:, None], (steps, LANES))

    obs_specs = [pl.BlockSpec((SUBS, rows, LANES), functools.partial(lambda h, i, o: (i, 0, h), h)) for h in range(halves)]
    s_send = pl.pallas_call(
        forward_kernel,
        out_shape=field,
        grid_spec=pltpu.PrefetchScalarGridSpec(
            num_scalar_prefetch=1,
            grid=(steps // SUBS,),
            in_specs=obs_specs
            + obs_specs
            + [
                smem,
                pl.BlockSpec((rows, cols), lambda i, o: (0, 0)),
                pl.BlockSpec((SUBS, LANES), lambda i, o: (i, 0)),
            ],
            out_specs=pl.BlockSpec((devices, strip, SUBS, cols), lambda i, o: (0, 0, i, 0)),
            scratch_shapes=[
                pltpu.VMEM((rows + 2, SUBS, cols), F32),
                pltpu.VMEM((rows, cols), F32),
            ],
        ),
        compiler_params=big,
        name="forward",
    )(order_arr, *([observations] * halves), *([obs_mask] * halves), class_kappa, range_class, prec)
    s = lax.all_to_all(s_send, AXES, 0, 0, tiled=True)

    slots = jnp.arange(total, dtype=jnp.int32) // steps
    own = jnp.where(slots == me, jnp.tile(obs_precision, devices), 0.0)
    every = global_sum(own.reshape(total // LANES, LANES), devices).reshape(total)
    dia = jnp.broadcast_to(every[:, None], (total, LANES))
    chunk = min(total, 256)
    hi, lo = pl.pallas_call(
        split_kernel,
        out_shape=[jax.ShapeDtypeStruct((total, total), BF16)] * 2,
        grid=(total // chunk,),
        in_specs=[pl.BlockSpec((chunk, total), lambda i: (i, 0))],
        out_specs=[pl.BlockSpec((chunk, total), lambda i: (i, 0))] * 2,
        name="split",
    )(time_precision)
    cls = lax.dynamic_slice_in_dim(range_class, my_strip * strip, strip, 0)

    one = lambda f: pl.BlockSpec((devices, 1, steps, cols), f)
    whole = pl.BlockSpec((total, total), lambda q: (0, 0), pipeline_mode=pl.Buffered(1))
    operands = [pltpu.VMEM((total, cols), BF16)] * 2
    u_send = pl.pallas_call(
        first_kernel,
        out_shape=field,
        grid=(strip,),
        in_specs=[whole, whole, one(lambda q: (0, q, 0, 0))],
        out_specs=one(lambda q: (0, q, 0, 0)),
        scratch_shapes=operands,
        compiler_params=big,
        name="first",
    )(hi, lo, s)
    u = lax.all_to_all(u_send, AXES, 0, 0, tiled=True)

    forth = [(order[k], order[k + 1]) for k in range(devices - 1)]
    back = [(b, a) for a, b in forth]
    up = lax.ppermute(u_send[:, strip - 1], AXES, forth)
    down = lax.ppermute(u_send[:, 0], AXES, back)
    edge = pl.BlockSpec((devices, steps, cols), lambda q: (0, 0, 0), pipeline_mode=pl.Buffered(1))
    v_send = pl.pallas_call(
        second_kernel,
        out_shape=field,
        grid=(strip,),
        in_specs=[
            whole,
            whole,
            smem,
            pl.BlockSpec((strip, cols), lambda q: (0, 0)),
            pl.BlockSpec((total, LANES), lambda q: (0, 0), pipeline_mode=pl.Buffered(1)),
            edge,
            edge,
            one(lambda q: (0, jnp.maximum(q - 1, 0), 0, 0)),
            one(lambda q: (0, q, 0, 0)),
            one(lambda q: (0, jnp.minimum(q + 1, strip - 1), 0, 0)),
            one(lambda q: (0, q, 0, 0)),
        ],
        out_specs=one(lambda q: (0, q, 0, 0)),
        scratch_shapes=operands,
        compiler_params=big,
        cost_estimate=pl.CostEstimate(flops=6 * total * total * strip * cols, bytes_accessed=20 * 2**20, transcendentals=0),
        name="second",
    )(hi, lo, class_kappa, cls, dia, up, down, u_send, u_send, u_send, s)
    v = lax.all_to_all(v_send, AXES, 0, 0, tiled=True)

    nat = pl.BlockSpec((SUBS, rows, LANES), lambda i, h, o: (i, 0, h))
    strips = pl.BlockSpec((devices, strip, SUBS, LANES), lambda i, h, o: (0, 0, i, h))
    row = pl.BlockSpec((SUBS, LANES), lambda i, h, o: (i, 0))
    fixed = lambda n: pl.BlockSpec((n * SUBS, LANES), lambda i, h, o: (0, 0))

    def local(kernel, name, specs, out_specs, out_shape, *args):
        return pl.pallas_call(
            kernel,
            out_shape=out_shape,
            grid_spec=pltpu.PrefetchScalarGridSpec(
                num_scalar_prefetch=1,
                grid=(steps // SUBS, halves),
                in_specs=[nat, nat, row] + specs,
                out_specs=out_specs,
            ),
            compiler_params=big,
            cost_estimate=pl.CostEstimate(flops=10**7, bytes_accessed=16 * 2**20, transcendentals=0),
            name=name,
        )(order_arr, observations, obs_mask, prec, *args)

    sums = local(moments_kernel, "moments", [strips], fixed(2), jax.ShapeDtypeStruct((2 * SUBS, LANES), F32), u)
    sums = global_sum(sums, devices)
    new = local(residual_kernel, "residual", [strips, fixed(2)], fixed(1), small, u, sums)
    new = global_sum(new, devices)
    d, part = local(
        direction_kernel, "direction", [strips, fixed(2), fixed(1)], [strips, fixed(1)], [field, small], u, sums, new
    )
    some = max(1, devices // 4)
    flat = pl.BlockSpec((some, strip, steps, cols), lambda i: (i, 0, 0, 0))
    den = pl.pallas_call(
        denominator_kernel,
        out_shape=small,
        grid=(devices // some,),
        in_specs=[flat, flat, pl.BlockSpec((2 * SUBS, LANES), lambda i: (0, 0)), pl.BlockSpec((SUBS, LANES), lambda i: (0, 0))],
        out_specs=pl.BlockSpec((SUBS, LANES), lambda i: (0, 0)),
        compiler_params=big,
        name="denominator",
    )(d, v, sums, part)
    den = global_sum(den, devices)
    return tuple(
        local(
            final_kernel,
            "final",
            [strips, strips, fixed(2), fixed(1), fixed(1)],
            [nat, nat],
            [jax.ShapeDtypeStruct(observations.shape, F32)] * 2,
            u,
            v,
            sums,
            new,
            den,
        )
    )


def per_device(*args):
    devices = lax.axis_size("tgrp") * lax.axis_size("inner")
    steps, rows, cols = args[0].shape
    total = args[5].shape[0]
    fits = (
        devices & (devices - 1) == 0
        and lax.axis_size("inner") % 2 == 0
        and rows % devices == 0
        and steps % SUBS == 0
        and cols % LANES == 0
        and total % 256 == 0
        and 64 % steps == 0
        and devices % 4 == 0
    )
    return (fast if fits else general)(*args)


def solution(mesh):
    return jax.shard_map(
        per_device,
        mesh=mesh,
        in_specs=(
            P(AXES, None, None),
            P(AXES, None, None),
            P(AXES),
            P(),
            P(),
            P(),
        ),
        out_specs=(P(AXES, None, None), P(AXES, None, None)),
        check_vma=False,
    )
```

```python
import functools

import jax
import jax.numpy as jnp
from jax import lax
from jax.experimental import pallas as pl
from jax.experimental.pallas import tpu as pltpu
from jax.sharding import PartitionSpec as P

ITERS = 2
LANES = 128
SUBS = 8
AXES = ("tgrp", "inner")
F32 = jnp.float32
BF16 = jnp.bfloat16


def spatial(field, kappa_sq):
    padded = jnp.pad(field, ((0, 0), (1, 1), (1, 1)))
    edges = padded[:, 2:, 1:-1] + padded[:, :-2, 1:-1] + padded[:, 1:-1, 2:] + padded[:, 1:-1, :-2]
    corners = padded[:, 2:, 2:] + padded[:, 2:, :-2] + padded[:, :-2, 2:] + padded[:, :-2, :-2]
    return (kappa_sq + 20.0 / 6.0) * field - (4.0 * edges + corners) / 6.0


def squares(residual):
    return lax.psum(jnp.sum(residual * residual), AXES)


def general(observations, obs_mask, obs_precision, range_class, class_kappa, time_precision):
    devices = lax.axis_size("tgrp") * lax.axis_size("inner")
    steps_dev, rows, cols = observations.shape
    remain = rows * cols // devices
    total_len = time_precision.shape[0]
    levels = jnp.arange(class_kappa.shape[0], dtype=jnp.int32)
    kappa_sq = jnp.sum(
        jnp.where(
            range_class[None, :, :] == levels[:, None, None], class_kappa[:, None, None], 0.0
        ),
        axis=0,
    )
    weight = obs_precision[:, None, None] * obs_mask.astype(F32)
    right_side = weight * observations
    solution_field = jnp.zeros_like(right_side)
    residual = right_side
    direction = right_side
    norm_now = squares(residual)
    for step in range(ITERS):
        blocks = spatial(direction, kappa_sq).reshape(steps_dev, devices, remain)
        moved = lax.all_to_all(blocks.transpose(1, 0, 2), AXES, 0, 0, tiled=True)
        product = jnp.dot(
            time_precision,
            moved.reshape(total_len, remain),
            precision=lax.Precision.HIGHEST,
            preferred_element_type=F32,
        )
        back = lax.all_to_all(product.reshape(devices, steps_dev, remain), AXES, 0, 0, tiled=True)
        image = back.transpose(1, 0, 2).reshape(steps_dev, rows, cols) + weight * direction
        alpha = norm_now / lax.psum(jnp.sum(direction * image), AXES)
        solution_field = solution_field + alpha * direction
        residual = residual - alpha * image
        if step + 1 < ITERS:
            norm_next = squares(residual)
            direction = residual + norm_next / norm_now * direction
            norm_now = norm_next
    return (solution_field, residual)


def strip_order(groups, members):
    ring = [g ^ (g >> 1) for g in range(groups)]
    order = []
    for plane in range(members // 2):
        for g in ring if plane % 2 == 0 else ring[::-1]:
            order += [g * members + plane * 2, g * members + plane * 2 + 1]
    return order


def global_sum(part, groups, members):
    devices = groups * members

    def stage(part, strides):
        def other(mask):
            return lax.ppermute(part, AXES, [(a, a ^ mask) for a in range(devices)])

        if len(strides) == 1:
            return part + other(strides[0])
        one, two = strides
        return (part + other(one)) + (other(two) + other(one | two))

    bits = [1 << k for k in range(devices.bit_length() - 1)]
    part = stage(part, bits[:1])
    for k in range(1, len(bits), 2):
        part = stage(part, bits[k : k + 2])
    return part


def kappa_of(classes, table_ref):
    field = jnp.zeros(classes.shape, F32)
    for level in range(table_ref.shape[0]):
        field = jnp.where(classes == level, table_ref[level], field)
    return field + 20.0 / 6.0


def neighbours(edge, centre, column, cols):
    both = 4.0 * centre + edge
    left = jnp.where(column == 0, 0.0, pltpu.roll(both, 1, both.ndim - 1))
    right = jnp.where(column == cols - 1, 0.0, pltpu.roll(both, cols - 1, both.ndim - 1))
    return 4.0 * edge + left + right


def forward_kernel(order_ref, *refs):
    s_ref, bt, kap = refs[-3:]
    table_ref, cls_ref, prec_ref = refs[-6:-3]
    halves = (len(refs) - 6) // 2
    obs, mask = refs[:halves], refs[halves : 2 * halves]
    devices, strip, subs, cols = s_ref.shape
    rows = devices * strip

    @pl.when(pl.program_id(0) == 0)
    def _():
        kap[...] = kappa_of(cls_ref[...], table_ref)
        bt[0] = jnp.zeros_like(bt[0])
        bt[rows + 1] = jnp.zeros_like(bt[0])

    prec = prec_ref[...]

    def load(k, carry):
        for q in range(strip):
            r = k * strip + q
            for h in range(halves):
                at = pl.ds(r, subs, stride=rows)
                o = obs[h].reshape(subs * rows, LANES)[at, :]
                m = mask[h].reshape(subs * rows, LANES)[at, :]
                bt[r + 1, :, h * LANES : (h + 1) * LANES] = prec * m.astype(F32) * o
        return carry

    lax.fori_loop(0, devices, load, 0)
    column = lax.broadcasted_iota(jnp.int32, (subs, cols), 1)

    def stencil(k, carry):
        dest = order_ref[k]
        for q in range(strip):
            r = k * strip + q
            centre = bt[r + 1]
            around = neighbours(bt[r] + bt[r + 2], centre, column, cols)
            s_ref[dest, q] = kap[pl.ds(r, 1), :] * centre - around * (1.0 / 6.0)
        return carry

    lax.fori_loop(0, devices, stencil, 0)


def split_kernel(t_ref, hi_ref, lo_ref):
    value = t_ref[...]
    hi = value.astype(BF16)
    hi_ref[...] = hi
    lo_ref[...] = (value - hi.astype(F32)).astype(BF16)


def times(hi_ref, lo_ref, xh, xl, out_ref):
    devices, _, steps, cols = out_ref.shape
    total = devices * steps
    tile = min(total, 256)

    def body(m, carry):
        at = pl.ds(pl.multiple_of(m * tile, tile), tile)
        hi, lo = hi_ref[at, :], lo_ref[at, :]
        dot = functools.partial(jnp.dot, preferred_element_type=F32)
        acc = dot(hi, xl[...]) + dot(lo, xh[...]) + dot(hi, xh[...])
        out_ref[pl.ds(m * (tile // steps), tile // steps), 0] = acc.reshape(tile // steps, steps, cols)
        return carry

    lax.fori_loop(0, total // tile, body, 0)


def first_kernel(hi_ref, lo_ref, s_ref, u_ref, xh, xl):
    devices, _, steps, cols = s_ref.shape
    value = s_ref[...].reshape(devices * steps, cols)
    hi = value.astype(BF16)
    xh[...] = hi
    xl[...] = (value - hi.astype(F32)).astype(BF16)
    times(hi_ref, lo_ref, xh, xl, u_ref)


def second_kernel(
    hi_ref, lo_ref, table_ref, cls_ref, dia_ref, up_ref, down_ref, above_ref, u_ref, below_ref, s_ref, v_ref, xh, xl
):
    q = pl.program_id(0)
    last = pl.num_programs(0) - 1
    devices, _, steps, cols = s_ref.shape
    kap = kappa_of(cls_ref[pl.ds(q, 1), :], table_ref)
    some = max(1, 64 // steps)
    size = some * steps
    column = lax.broadcasted_iota(jnp.int32, (size, cols), 1)

    def body(i, carry):
        at = pl.ds(i * some, some)
        flat = lambda value: value.reshape(size, cols)
        above = jnp.where(q == 0, flat(up_ref[at]), flat(above_ref[at, 0]))
        below = jnp.where(q == last, flat(down_ref[at]), flat(below_ref[at, 0]))
        centre = flat(u_ref[at, 0])
        rows = pl.ds(pl.multiple_of(i * size, size), size)
        dia = dia_ref[rows, :]
        dia = jnp.concatenate([dia] * (cols // LANES), axis=1)
        value = kap * centre - neighbours(above + below, centre, column, cols) * (1.0 / 6.0)
        value = value + dia * flat(s_ref[at, 0])
        hi = value.astype(BF16)
        xh[rows, :] = hi
        xl[rows, :] = (value - hi.astype(F32)).astype(BF16)
        return carry

    lax.fori_loop(0, devices // some, body, 0)
    times(hi_ref, lo_ref, xh, xl, v_ref)


def total_of(ref, at=0):
    return jnp.sum(ref[at * SUBS : (at + 1) * SUBS, :], keepdims=True)


def each_row(order_ref, obs_ref, mask_ref, prec_ref, fields, body, carry):
    devices, strip, subs, _ = fields.shape
    rows = devices * strip
    prec = prec_ref[...]

    def one(k, carry):
        dest = order_ref[k]
        for q in range(strip):
            at = pl.ds(k * strip + q, subs, stride=rows)
            weight = prec * mask_ref.reshape(subs * rows, LANES)[at, :].astype(F32)
            b = weight * obs_ref.reshape(subs * rows, LANES)[at, :]
            z = fields[dest, q] + prec * b
            carry = body(at, dest, q, b, z, weight, carry)
        return carry

    return lax.fori_loop(0, devices, one, carry)


def is_first():
    return jnp.logical_and(pl.program_id(0) == 0, pl.program_id(1) == 0)


def moments_kernel(order_ref, obs_ref, mask_ref, prec_ref, u_ref, sums_ref):
    @pl.when(is_first())
    def _():
        sums_ref[...] = jnp.zeros_like(sums_ref)

    def body(at, dest, q, b, z, weight, carry):
        return carry[0] + b * b, carry[1] + b * z

    zero = jnp.zeros((SUBS, LANES), F32)
    bb, bz = each_row(order_ref, obs_ref, mask_ref, prec_ref, u_ref, body, (zero, zero))
    sums_ref[:SUBS] += bb
    sums_ref[SUBS:] += bz


def residual_kernel(order_ref, obs_ref, mask_ref, prec_ref, u_ref, sums_ref, out_ref):
    @pl.when(is_first())
    def _():
        out_ref[...] = jnp.zeros_like(out_ref)

    alpha = total_of(sums_ref) / total_of(sums_ref, 1)

    def body(at, dest, q, b, z, weight, carry):
        r1 = b - alpha * z
        return carry + r1 * r1

    zero = jnp.zeros((SUBS, LANES), F32)
    out_ref[...] += each_row(order_ref, obs_ref, mask_ref, prec_ref, u_ref, body, zero)


def direction_kernel(order_ref, obs_ref, mask_ref, prec_ref, u_ref, sums_ref, new_ref, d_ref, out_ref):
    @pl.when(is_first())
    def _():
        out_ref[...] = jnp.zeros_like(out_ref)

    alpha = total_of(sums_ref) / total_of(sums_ref, 1)
    beta = total_of(new_ref) / total_of(sums_ref)

    def body(at, dest, q, b, z, weight, carry):
        d1 = b - alpha * z + beta * b
        d_ref[dest, q] = d1
        return carry + d1 * ((1.0 + beta) * z - alpha * (weight * z))

    zero = jnp.zeros((SUBS, LANES), F32)
    out_ref[...] += each_row(order_ref, obs_ref, mask_ref, prec_ref, u_ref, body, zero)


def denominator_kernel(d_ref, v_ref, sums_ref, part_ref, out_ref):
    @pl.when(pl.program_id(0) == 0)
    def _():
        out_ref[...] = part_ref[...]

    alpha = total_of(sums_ref) / total_of(sums_ref, 1)
    product = d_ref[...] * v_ref[...]
    product = product.reshape(-1, SUBS, product.shape[-1]).sum(0)
    acc = product[:, :LANES]
    for h in range(1, product.shape[-1] // LANES):
        acc = acc + product[:, h * LANES : (h + 1) * LANES]
    out_ref[...] -= alpha * acc


def final_kernel(
    order_ref, obs_ref, mask_ref, prec_ref, u_ref, v_ref, sums_ref, new_ref, den_ref, x_ref, r_ref
):
    alpha = total_of(sums_ref) / total_of(sums_ref, 1)
    beta = total_of(new_ref) / total_of(sums_ref)
    step = total_of(new_ref) / total_of(den_ref)
    subs, rows, _ = x_ref.shape

    def body(at, dest, q, b, z, weight, carry):
        r1 = b - alpha * z
        d1 = r1 + beta * b
        image = (1.0 + beta) * z - alpha * (v_ref[dest, q] + weight * z)
        x_ref.reshape(subs * rows, LANES)[at, :] = alpha * b + step * d1
        r_ref.reshape(subs * rows, LANES)[at, :] = r1 - step * image
        return carry

    each_row(order_ref, obs_ref, mask_ref, prec_ref, u_ref, body, 0)


def fast(observations, obs_mask, obs_precision, range_class, class_kappa, time_precision):
    groups, members = lax.axis_size("tgrp"), lax.axis_size("inner")
    devices = groups * members
    steps, rows, cols = observations.shape
    total = time_precision.shape[0]
    strip = rows // devices
    halves = cols // LANES
    order = strip_order(groups, members)
    order_arr = jnp.array(order, jnp.int32)
    place = [order.index(d) for d in range(devices)]
    me = lax.axis_index(AXES)
    my_strip = jnp.array(place, jnp.int32)[me]
    field = jax.ShapeDtypeStruct((devices, strip, steps, cols), F32)
    small = jax.ShapeDtypeStruct((SUBS, LANES), F32)
    smem = pl.BlockSpec(memory_space=pltpu.SMEM)
    big = pltpu.CompilerParams(vmem_limit_bytes=60 * 2**20)

    prec = jnp.broadcast_to(obs_precision[:, None], (steps, LANES))

    obs_specs = [pl.BlockSpec((SUBS, rows, LANES), functools.partial(lambda h, i, o: (i, 0, h), h)) for h in range(halves)]
    s_send = pl.pallas_call(
        forward_kernel,
        out_shape=field,
        grid_spec=pltpu.PrefetchScalarGridSpec(
            num_scalar_prefetch=1,
            grid=(steps // SUBS,),
            in_specs=obs_specs
            + obs_specs
            + [
                smem,
                pl.BlockSpec((rows, cols), lambda i, o: (0, 0)),
                pl.BlockSpec((SUBS, LANES), lambda i, o: (i, 0)),
            ],
            out_specs=pl.BlockSpec((devices, strip, SUBS, cols), lambda i, o: (0, 0, i, 0)),
            scratch_shapes=[
                pltpu.VMEM((rows + 2, SUBS, cols), F32),
                pltpu.VMEM((rows, cols), F32),
            ],
        ),
        compiler_params=big,
        name="forward",
    )(order_arr, *([observations] * halves), *([obs_mask] * halves), class_kappa, range_class, prec)
    s = lax.all_to_all(s_send, AXES, 0, 0, tiled=True)

    slots = jnp.arange(total, dtype=jnp.int32) // steps
    own = jnp.where(slots == me, jnp.tile(obs_precision, devices), 0.0)
    every = global_sum(own.reshape(total // LANES, LANES), groups, members).reshape(total)
    dia = jnp.broadcast_to(every[:, None], (total, LANES))
    chunk = min(total, 256)
    hi, lo = pl.pallas_call(
        split_kernel,
        out_shape=[jax.ShapeDtypeStruct((total, total), BF16)] * 2,
        grid=(total // chunk,),
        in_specs=[pl.BlockSpec((chunk, total), lambda i: (i, 0))],
        out_specs=[pl.BlockSpec((chunk, total), lambda i: (i, 0))] * 2,
        name="split",
    )(time_precision)
    cls = lax.dynamic_slice_in_dim(range_class, my_strip * strip, strip, 0)

    s, dia = lax.optimization_barrier((s, dia))
    one = lambda f: pl.BlockSpec((devices, 1, steps, cols), f)
    whole = pl.BlockSpec((total, total), lambda q: (0, 0), pipeline_mode=pl.Buffered(1))
    operands = [pltpu.VMEM((total, cols), BF16)] * 2
    u_send = pl.pallas_call(
        first_kernel,
        out_shape=field,
        grid=(strip,),
        in_specs=[whole, whole, one(lambda q: (0, q, 0, 0))],
        out_specs=one(lambda q: (0, q, 0, 0)),
        scratch_shapes=operands,
        compiler_params=big,
        name="first",
    )(hi, lo, s)

    forth = [(order[k], order[k + 1]) for k in range(devices - 1)]
    back = [(b, a) for a, b in forth]
    up = lax.ppermute(u_send[:, strip - 1], AXES, forth)
    down = lax.ppermute(u_send[:, 0], AXES, back)
    u_send, up, down = lax.optimization_barrier((u_send, up, down))
    u = lax.all_to_all(u_send, AXES, 0, 0, tiled=True)
    edge = pl.BlockSpec((devices, steps, cols), lambda q: (0, 0, 0), pipeline_mode=pl.Buffered(1))
    v_send = pl.pallas_call(
        second_kernel,
        out_shape=field,
        grid=(strip,),
        in_specs=[
            whole,
            whole,
            smem,
            pl.BlockSpec((strip, cols), lambda q: (0, 0)),
            pl.BlockSpec((total, LANES), lambda q: (0, 0), pipeline_mode=pl.Buffered(1)),
            edge,
            edge,
            one(lambda q: (0, jnp.maximum(q - 1, 0), 0, 0)),
            one(lambda q: (0, q, 0, 0)),
            one(lambda q: (0, jnp.minimum(q + 1, strip - 1), 0, 0)),
            one(lambda q: (0, q, 0, 0)),
        ],
        out_specs=one(lambda q: (0, q, 0, 0)),
        scratch_shapes=operands,
        compiler_params=big,
        cost_estimate=pl.CostEstimate(flops=6 * total * total * strip * cols, bytes_accessed=20 * 2**20, transcendentals=0),
        name="second",
    )(hi, lo, class_kappa, cls, dia, up, down, u_send, u_send, u_send, s)
    v = lax.all_to_all(v_send, AXES, 0, 0, tiled=True)

    nat = pl.BlockSpec((SUBS, rows, LANES), lambda i, h, o: (i, 0, h))
    strips = pl.BlockSpec((devices, strip, SUBS, LANES), lambda i, h, o: (0, 0, i, h))
    row = pl.BlockSpec((SUBS, LANES), lambda i, h, o: (i, 0))
    fixed = lambda n: pl.BlockSpec((n * SUBS, LANES), lambda i, h, o: (0, 0))

    def local(kernel, name, specs, out_specs, out_shape, *args):
        return pl.pallas_call(
            kernel,
            out_shape=out_shape,
            grid_spec=pltpu.PrefetchScalarGridSpec(
                num_scalar_prefetch=1,
                grid=(steps // SUBS, halves),
                in_specs=[nat, nat, row] + specs,
                out_specs=out_specs,
            ),
            compiler_params=big,
            cost_estimate=pl.CostEstimate(flops=10**7, bytes_accessed=16 * 2**20, transcendentals=0),
            name=name,
        )(order_arr, observations, obs_mask, prec, *args)

    sums = local(moments_kernel, "moments", [strips], fixed(2), jax.ShapeDtypeStruct((2 * SUBS, LANES), F32), u)
    sums = global_sum(sums, groups, members)
    new = local(residual_kernel, "residual", [strips, fixed(2)], fixed(1), small, u, sums)
    new = global_sum(new, groups, members)
    d, part = local(
        direction_kernel, "direction", [strips, fixed(2), fixed(1)], [strips, fixed(1)], [field, small], u, sums, new
    )
    some = max(1, devices // 4)
    flat = pl.BlockSpec((some, strip, steps, cols), lambda i: (i, 0, 0, 0))
    den = pl.pallas_call(
        denominator_kernel,
        out_shape=small,
        grid=(devices // some,),
        in_specs=[flat, flat, pl.BlockSpec((2 * SUBS, LANES), lambda i: (0, 0)), pl.BlockSpec((SUBS, LANES), lambda i: (0, 0))],
        out_specs=pl.BlockSpec((SUBS, LANES), lambda i: (0, 0)),
        compiler_params=big,
        name="denominator",
    )(d, v, sums, part)
    den = global_sum(den, groups, members)
    return tuple(
        local(
            final_kernel,
            "final",
            [strips, strips, fixed(2), fixed(1), fixed(1)],
            [nat, nat],
            [jax.ShapeDtypeStruct(observations.shape, F32)] * 2,
            u,
            v,
            sums,
            new,
            den,
        )
    )


def per_device(*args):
    devices = lax.axis_size("tgrp") * lax.axis_size("inner")
    steps, rows, cols = args[0].shape
    total = args[5].shape[0]
    fits = (
        devices & (devices - 1) == 0
        and lax.axis_size("inner") % 2 == 0
        and rows % devices == 0
        and steps % SUBS == 0
        and cols % LANES == 0
        and total % 256 == 0
        and 64 % steps == 0
        and devices % 4 == 0
    )
    return (fast if fits else general)(*args)


def solution(mesh):
    return jax.shard_map(
        per_device,
        mesh=mesh,
        in_specs=(
            P(AXES, None, None),
            P(AXES, None, None),
            P(AXES),
            P(),
            P(),
            P(),
        ),
        out_specs=(P(AXES, None, None), P(AXES, None, None)),
        check_vma=False,
    )
```
